32 devices in a mesh: row: 4 (over y, core), blk: 8 (over z, x).
Axes of the slice: x: 2, y: 2, z: 4, core: 2. Of those that a mesh axis runs over, the one named last changes fastest.
Arguments:
- right_side: float32 [4, 8, 8, 32, 256], P('row', 'blk')
- noise_level: float32 [4, 8, 8, 256], P('row', 'blk'), may hold values from 3 to 6
- near_blocks: bfloat16 [4, 8, 8, 9, 256, 256], P('row', 'blk'), as said below
- skeleton_basis: bfloat16 [4, 8, 8, 64, 256], P('row', 'blk'), may hold values from -0.125 to 0.125
- skeleton_index: int32 [4, 8, 64], P('row', 'blk'), may hold values from 0 to 2047, as said below
- far_list: int32 [4, 8, 7], P('row', 'blk'), may hold values from 0 to 7, as said below
- couplings: bfloat16 [4, 8, 7, 64, 64], P('row', 'blk'), as said below
Outputs:
- solution: float32 [4, 8, 8, 32, 256], P('row', 'blk')
- residual: float32 [4, 8, 8, 32, 256], P('row', 'blk')
- quadratic: float32 [32], replicated
The draws below stay inside these ranges and needn't reach their ends.
Inputs may be any that keep to these rules, and one draw needn't show every extreme that they name: `far_list`: each device's 7 entries are distinct, none is the device's own blk index, and the two cyclic neighbours along blk are always among them; box b lists box b' exactly when b' lists b, and within a row every box's far boxes lie at the same set of cyclic offsets from its own index. `couplings`: the coupling that box b holds for far box b' is the transpose of the one that b' holds for b. `near_blocks`: A leaf's block for near slot s is the transpose of the block that its slot-s neighbour holds for slot 8 - s; slot 4 blocks are symmetric. `skeleton_index`: each device's 64 entries are distinct tracers of its 2048.
All inputs are finite; a program needn't handle non-finite values.
Results may differ from the reference program's by a relative error of at most 0.03.
Values may be sent and summed in bfloat16 or wider, within the bound.
A program may use at most 64 MiB of HBM per device.

```python
import math
import jax
import jax.numpy as jnp

LEAF = 256
SKEL = 64
RHS = 32
NEAR = 9
ITERS = 4
LEAF_ROWS = 2
LEAF_COLS = 4
LEAF_DEV = 8
FAR = 7
POINTS = 65536
N_ROW = 4
N_BLK = 8


def draw_right_side(key, part):
    first_key, second_key = jax.random.split(key, 2)
    shape = (N_ROW, N_BLK, LEAF_DEV, RHS, LEAF)
    device_count = N_ROW * N_BLK
    device_order = jnp.arange(device_count, dtype=jnp.float32).reshape(N_ROW, N_BLK)
    device_ramp = 3.0 ** (device_order / (device_count - 1))
    column_scale = jnp.exp(jax.random.uniform(second_key, (RHS,), jnp.float32, math.log(0.3), math.log(3.0)))
    base = jax.random.normal(first_key, shape, jnp.float32)
    return base * device_ramp[:, :, None, None, None] * column_scale[None, None, None, :, None]


def draw_near_blocks(key, part):
    grid_rows = N_ROW * LEAF_ROWS
    grid_cols = N_BLK * LEAF_COLS
    scale = 4.0 * (8.0 * NEAR * LEAF) ** (-0.5)
    shape = (grid_rows, grid_cols, LEAF, LEAF)
    own = jax.random.normal(jax.random.fold_in(key, 41), shape, jnp.float32)
    own = (own + jnp.swapaxes(own, -1, -2)) * 0.70710678 * scale
    own = own + 3.0 * jnp.eye(LEAF, dtype=jnp.float32)[None, None, :, :]
    slots = [own] * 9
    forward = ((5, 0, 1), (6, 1, -1), (7, 1, 0), (8, 1, 1))
    for slot_index, step_row, step_col in forward:
        block = jax.random.normal(jax.random.fold_in(key, 50 + slot_index), shape, jnp.float32) * scale
        slots[slot_index] = block
        slots[8 - slot_index] = jnp.swapaxes(jnp.roll(block, (step_row, step_col), axis=(0, 1)), -1, -2)
    stacked = jnp.stack(slots, axis=2)
    stacked = stacked.reshape(N_ROW, LEAF_ROWS, N_BLK, LEAF_COLS, NEAR, LEAF, LEAF)
    stacked = jnp.moveaxis(stacked, 2, 1)
    return stacked.reshape(N_ROW, N_BLK, LEAF_ROWS * LEAF_COLS, NEAR, LEAF, LEAF).astype(jnp.bfloat16)


def draw_skeleton_index(key, part):
    points = LEAF_DEV * LEAF
    scores = jax.random.randint(jax.random.fold_in(key, 11), (N_ROW, N_BLK, points), 0, 2 ** 30 // points)
    scores = scores * points + jnp.arange(points, dtype=jnp.int32)[None, None, :]
    ordering = jnp.argsort(scores, axis=-1)
    return ordering[:, :, :SKEL].astype(jnp.int32)


def far_structure(key):
    half = N_BLK // 2
    pairs = (FAR - 1) // 2
    candidates = max(half - 2, 1)
    scores = jax.random.randint(jax.random.fold_in(key, 23), (N_ROW, candidates), 0, 2 ** 30 // candidates)
    scores = scores * candidates + jnp.arange(candidates, dtype=jnp.int32)[None, :]
    drawn = (2 + jnp.argsort(scores, axis=-1)[:, :pairs - 1]).astype(jnp.int32)
    nearest = jnp.ones((N_ROW, 1), jnp.int32)
    chosen = jnp.concatenate([nearest, drawn], axis=1).astype(jnp.int32)
    middle = jnp.full((N_ROW, 1), half, jnp.int32)
    offsets = jnp.concatenate([chosen, middle, N_BLK - chosen], axis=1).astype(jnp.int32)
    order_scores = jax.random.randint(jax.random.fold_in(key, 29), (N_ROW, N_BLK, FAR), 0, 2 ** 30 // FAR)
    order_scores = order_scores * FAR + jnp.arange(FAR, dtype=jnp.int32)[None, None, :]
    ordering = jnp.argsort(order_scores, axis=-1).astype(jnp.int32)
    return (offsets, ordering)


def draw_far_list(key, part):
    offsets, ordering = far_structure(key)
    row_index = jnp.arange(N_ROW, dtype=jnp.int32)[:, None, None]
    picked = offsets[row_index, ordering]
    own_index = jnp.arange(N_BLK, dtype=jnp.int32)[None, :, None]
    return ((own_index + picked) % N_BLK).astype(jnp.int32)


def draw_couplings(key, part):
    offsets, ordering = far_structure(key)
    half = N_BLK // 2
    pairs = (FAR - 1) // 2
    scale = 1.5 * (8.0 * FAR * SKEL) ** (-0.5)
    base = jax.random.normal(jax.random.fold_in(key, 31), (N_ROW, N_BLK, pairs + 1, SKEL, SKEL), jnp.float32) * scale
    positive = base[:, :, :pairs]
    centre = base[:, :, pairs]
    lower = jnp.arange(N_BLK, dtype=jnp.int32)[None, :, None, None] < half
    centre = jnp.where(lower, centre, jnp.swapaxes(jnp.roll(centre, half, axis=1), -1, -2))
    row_index = jnp.arange(N_ROW, dtype=jnp.int32)[:, None, None]
    partner = (jnp.arange(N_BLK, dtype=jnp.int32)[None, :, None] - offsets[:, None, :pairs]) % N_BLK
    pair_index = jnp.arange(pairs, dtype=jnp.int32)[None, None, :]
    negative = jnp.swapaxes(positive[row_index, partner, pair_index], -1, -2)
    canonical = jnp.concatenate([positive, centre[:, :, None], negative], axis=2)
    blk_index = jnp.arange(N_BLK, dtype=jnp.int32)[None, :, None]
    return canonical[row_index, blk_index, ordering].astype(jnp.bfloat16)


def shard_levels(key, shape, pieces, low, top_value):
    loudness, own = 1.0, jax.random.fold_in(key, 6)
    for dim, blocks in pieces:
        draws = jnp.exp(jax.random.uniform(jax.random.fold_in(own, dim), (blocks,), jnp.float32, low / len(pieces), top_value / len(pieces)))
        loudness = loudness * jnp.repeat(draws, shape[dim] // blocks).reshape([-1 if axis == dim else 1 for axis in range(len(shape))])
    return loudness


def normal_values(rng, dims, scale, reach, cuts=(), kind=jnp.bfloat16):
    entries = scale * jax.random.normal(rng, dims, jnp.float32)
    if cuts:
        entries = entries * shard_levels(rng, dims, cuts, -0.22, 0.18)
    return jnp.clip(entries, -reach, reach).astype(kind)


def setup_inputs(seed: int = 0) -> dict:
    seeds = jax.random.split(jax.random.key(seed), 8)
    return {
        "right_side": draw_right_side(jax.random.fold_in(seeds[7], 71), 0),
        "noise_level": jnp.clip(jnp.exp(math.log(6.0) - 0.6931472 * jax.random.uniform(seeds[1], (N_ROW, N_BLK, LEAF_DEV, LEAF), jnp.float32) ** shard_levels(seeds[1], (N_ROW, N_BLK, LEAF_DEV, LEAF), ((0, 4), (1, 8)), -0.2, 0.2)), 3.0, 6.0),
        "near_blocks": draw_near_blocks(jax.random.fold_in(seeds[7], 71), 0),
        "skeleton_basis": normal_values(seeds[3], (N_ROW, N_BLK, LEAF_DEV, SKEL, LEAF), (LEAF_DEV * LEAF) ** -0.5, 0.125, ((0, 4), (1, 8))),
        "skeleton_index": draw_skeleton_index(jax.random.fold_in(seeds[7], 71), 0),
        "far_list": draw_far_list(jax.random.fold_in(seeds[7], 71), 0),
        "couplings": draw_couplings(jax.random.fold_in(seeds[7], 71), 0),
    }


def to_grid(values):
    rest = values.shape[3:]
    shaped = values.reshape((N_ROW, N_BLK, LEAF_ROWS, LEAF_COLS) + rest)
    shaped = jnp.moveaxis(shaped, 2, 1)
    return shaped.reshape((N_ROW * LEAF_ROWS, N_BLK * LEAF_COLS) + rest)


def from_grid(values):
    rest = values.shape[2:]
    shaped = values.reshape((N_ROW, LEAF_ROWS, N_BLK, LEAF_COLS) + rest)
    shaped = jnp.moveaxis(shaped, 1, 2)
    return shaped.reshape((N_ROW, N_BLK, LEAF_ROWS * LEAF_COLS) + rest)


def skeleton_weights(rounded_dev, basis_dev, skeleton_dev):
    points = rounded_dev.shape[2]
    owner_leaf = skeleton_dev // points
    owner_point = skeleton_dev % points
    picked = rounded_dev[owner_leaf, :, owner_point].astype(jnp.float32)
    spread = jnp.einsum('lci,lki->ck', rounded_dev.astype(jnp.float32), basis_dev.astype(jnp.float32))
    return picked.T + spread


def spread_far(far_sum, basis_dev, skeleton_dev):
    points = basis_dev.shape[2]
    owner_leaf = skeleton_dev // points
    owner_point = skeleton_dev % points
    far_rounded = far_sum.astype(jnp.bfloat16).astype(jnp.float32)
    result = jnp.einsum('ck,lki->lci', far_rounded, basis_dev.astype(jnp.float32))
    return result.at[owner_leaf, :, owner_point].add(far_sum.T)


def apply_operator(direction, noise_level, grid_blocks, skeleton_basis, skeleton_index, far_list, couplings):
    rounded = direction.astype(jnp.bfloat16)
    n_rows = rounded.shape[0]
    field = to_grid(rounded)
    near = jnp.zeros(field.shape, jnp.float32)
    for slot_index in range(9):
        shift_row = 1 - slot_index // 3
        shift_col = 1 - slot_index % 3
        sources = jnp.roll(field, (shift_row, shift_col), axis=(0, 1))
        near = near + jnp.einsum('xyci,xyij->xycj', sources.astype(jnp.float32), grid_blocks[:, :, slot_index].astype(jnp.float32))
    result = from_grid(near)
    skeleton = jax.vmap(jax.vmap(skeleton_weights))(rounded, skeleton_basis, skeleton_index)
    skeleton_rounded = skeleton.astype(jnp.bfloat16)
    selected = skeleton_rounded[jnp.arange(n_rows)[:, None, None], far_list]
    far_sum = jnp.einsum('rbjck,rbjkm->rbcm', selected.astype(jnp.float32), couplings.astype(jnp.float32))
    result = result + jax.vmap(jax.vmap(spread_far))(far_sum, skeleton_basis, skeleton_index)
    return noise_level[:, :, :, None, :] * direction + result


def reference(right_side, noise_level, near_blocks, skeleton_basis, skeleton_index, far_list, couplings):
    grid_blocks = to_grid(near_blocks)

    def operate(field):
        return apply_operator(field, noise_level, grid_blocks, skeleton_basis, skeleton_index, far_list, couplings)

    axes = (0, 1, 2, 4)
    solution = jnp.zeros_like(right_side)
    residual = right_side
    direction = right_side
    norm_now = jnp.sum(residual * residual, axis=axes)
    for step_index in range(ITERS):
        applied = operate(direction)
        step_size = norm_now / jnp.sum(direction * applied, axis=axes)
        solution = solution + step_size[:, None] * direction
        residual = residual - step_size[:, None] * applied
        norm_next = jnp.sum(residual * residual, axis=axes)
        direction = residual + (norm_next / norm_now)[:, None] * direction
        norm_now = norm_next
    quadratic = jnp.sum(right_side * solution, axis=axes) / POINTS
    return solution, residual, quadratic
```

```python
import functools

import jax
import jax.numpy as jnp
from jax import lax
from jax.experimental import pallas as pl
from jax.experimental.pallas import tpu as pltpu
from jax.sharding import PartitionSpec as P

ITERS = 4
LEAF_ROWS = 2
LEAF_COLS = 4
MESH = pl.DeviceIdType.MESH
HIGHEST = lax.Precision.HIGHEST
SHIFTS = ((-1, 0), (1, 0), (0, -1), (0, 1), (-1, -1), (-1, 1), (1, -1), (1, 1))


def span(shift, count, incoming):
    if shift == 0:
        return 1, count
    if incoming:
        return (0 if shift > 0 else count + 1), 1
    return (count if shift > 0 else 1), 1


def each(count, body):
    if count <= 16:
        for i in range(count):
            body(i)
    else:
        pl.loop(0, count)(body)


def kernel(
    n_row, n_blk, tracers,
    right_ref, noise_ref, blocks_hbm, basis_ref, index_ref, far_ref, coupling_ref,
    solution_ref, residual_ref, quadratic_ref,
    blocks, mixed, extended, direction, applied, skeletons, row_sums, blk_sums,
    load_sem, halo_send, halo_recv, skel_send, skel_recv, row_send, row_recv, blk_send, blk_recv,
):
    leaves, columns, width = right_ref.shape
    rank = basis_ref.shape[1]
    far_count = coupling_ref.shape[0]
    my_row, my_blk = lax.axis_index("row"), lax.axis_index("blk")

    loads = [
        pltpu.make_async_copy(blocks_hbm.at[l], blocks.at[l], load_sem.at[l]) for l in range(leaves)
    ]
    for load in loads:
        load.start()

    def row_at(o):
        return lax.rem(my_row + (o + n_row), n_row)

    def blk_at(o):
        return lax.rem(my_blk + (o + n_blk), n_blk)

    barrier = pltpu.get_barrier_semaphore()

    def greet(row, blk):
        pl.semaphore_signal(barrier, inc=1, device_id={"row": row, "blk": blk}, device_id_type=MESH)

    for o in range(1, n_row):
        greet(row_at(o), my_blk)
    each(n_blk - 1, lambda i: greet(my_row, blk_at(i + 1)))
    for dr, dc in SHIFTS[4:]:
        greet(row_at(dr), blk_at(dc))

    sublane = lax.broadcasted_iota(jnp.int32, (rank, rank), 0)
    lane = lax.broadcasted_iota(jnp.int32, (rank, rank), 1)
    as_row = jnp.broadcast_to(index_ref[...].astype(jnp.float32), (rank, rank))
    as_column = jnp.sum(jnp.where(sublane == lane, as_row, 0.0), axis=1, keepdims=True)
    point = lax.broadcasted_iota(jnp.int32, (rank, width), 1).astype(jnp.float32)
    for l in range(leaves):
        picks = jnp.where(point + float(width * l) == as_column, 1.0, 0.0).astype(jnp.bfloat16)
        mixed[l, :rank] = basis_ref[l]
        mixed[l, rank : 2 * rank] = picks
        mixed[l, 2 * rank :] = picks
        value = right_ref[l]
        direction[l] = value
        residual_ref[l] = value
        solution_ref[l] = jnp.zeros_like(value)
    quadratic_ref[...] = jnp.zeros_like(quadratic_ref)

    pl.semaphore_wait(barrier, (n_row - 1) + (n_blk - 1) + 4)

    ones = jnp.ones((8, 128), jnp.float32)
    head = lax.broadcasted_iota(jnp.int32, (8, columns), 0)
    spread_row = lax.broadcasted_iota(jnp.int32, (columns, 128), 0)
    spread_lane = lax.broadcasted_iota(jnp.int32, (columns, 128), 1)

    def halo(k, n):
        dr, dc = SHIFTS[n]
        (sr, nr), (sc, nc) = span(dr, LEAF_ROWS, False), span(dc, LEAF_COLS, False)
        (tr, _), (tc, _) = span(dr, LEAF_ROWS, True), span(dc, LEAF_COLS, True)
        return pltpu.make_async_remote_copy(
            src_ref=extended.at[k, pl.ds(sr, nr), pl.ds(sc, nc)],
            dst_ref=extended.at[k, pl.ds(tr, nr), pl.ds(tc, nc)],
            send_sem=halo_send.at[k, n],
            recv_sem=halo_recv.at[k, n],
            device_id={"row": row_at(dr), "blk": blk_at(dc)},
            device_id_type=MESH,
        )

    def row_copy(k, o):
        return pltpu.make_async_remote_copy(
            src_ref=row_sums.at[k, my_row],
            dst_ref=row_sums.at[k, my_row],
            send_sem=row_send.at[k, o - 1],
            recv_sem=row_recv.at[k, o - 1],
            device_id={"row": row_at(o), "blk": my_blk},
            device_id_type=MESH,
        )

    def blk_copy(buffer, send, recv, k, o):
        return pltpu.make_async_remote_copy(
            src_ref=buffer.at[k, my_blk],
            dst_ref=buffer.at[k, my_blk],
            send_sem=send.at[k],
            recv_sem=recv.at[k],
            device_id={"row": my_row, "blk": blk_at(o)},
            device_id_type=MESH,
        )

    def blk_wait(buffer, sem, k):
        every = buffer.at[k, pl.ds(0, n_blk - 1)]
        pltpu.make_async_copy(every, every, sem.at[k]).wait()

    def slots(l):
        a, c = divmod(l, LEAF_COLS)
        for s in range(9):
            yield s, a + s // 3, c + s % 3

    def inside(row, col):
        return 1 <= row <= LEAF_ROWS and 1 <= col <= LEAF_COLS

    def iteration(k, first):
        for l in range(leaves):
            a, c = divmod(l, LEAF_COLS)
            extended[k, a + 1, c + 1] = direction[l].astype(jnp.bfloat16)
        for n in range(8):
            halo(k, n).start()

        def field(row, col):
            return extended[k, row, col]

        both = jnp.zeros((columns, 2 * rank), jnp.float32)
        for l in range(leaves):
            a, c = divmod(l, LEAF_COLS)
            both = both + lax.dot_general(
                field(a + 1, c + 1), mixed[l, : 2 * rank], (((1,), (1,)), ((), ())),
                preferred_element_type=jnp.float32,
            )
        skeletons[k, my_blk] = (both[:, :rank] + both[:, rank:]).astype(jnp.bfloat16)
        each(n_blk - 1, lambda i: blk_copy(skeletons, skel_send, skel_recv, k, i + 1).start())

        for l in range(leaves):
            if first:
                loads[l].wait()
            total = noise_ref[l : l + 1] * direction[l]
            for s, row, col in slots(l):
                if inside(row, col):
                    total = total + jnp.dot(
                        field(row, col), blocks[l, s], preferred_element_type=jnp.float32
                    )
            applied[l] = total

        blk_wait(skeletons, skel_recv, k)
        far = jnp.zeros((columns, rank), jnp.float32)
        for j in range(far_count):
            far = far + jnp.dot(
                skeletons[k, far_ref[0, j]], coupling_ref[j], preferred_element_type=jnp.float32
            )
        far_high = far.astype(jnp.bfloat16)
        far_low = (far - far_high.astype(jnp.float32)).astype(jnp.bfloat16)
        far_all = jnp.concatenate([far_high, far_high, far_low], axis=1)

        for n in range(8):
            halo(k, n).wait_recv()

        sums = [jnp.zeros((columns, 128), jnp.float32) for _ in range(5)]
        for l in range(leaves):
            total = applied[l] + jnp.dot(far_all, mixed[l], preferred_element_type=jnp.float32)
            for s, row, col in slots(l):
                if not inside(row, col):
                    total = total + jnp.dot(
                        field(row, col), blocks[l, s], preferred_element_type=jnp.float32
                    )
            applied[l] = total
            d, r = direction[l], residual_ref[l]
            for q, product in enumerate((d * total, r * total, total * total, right_ref[l] * d, r * r)):
                for h in range(width // 128):
                    sums[q] = sums[q] + product[:, 128 * h : 128 * (h + 1)]

        part = jnp.zeros((8, columns), jnp.float32)
        for q in range(5):
            line = lax.dot_general(
                ones, sums[q], (((1,), (1,)), ((), ())),
                precision=HIGHEST, preferred_element_type=jnp.float32,
            )
            part = jnp.where(head == q, line, part)
        row_sums[k, my_row] = jnp.concatenate(
            [part, jnp.zeros((8, 128 - columns), jnp.float32)], axis=1
        )
        for o in range(1, n_row):
            row_copy(k, o).start()
        for o in range(1, n_row):
            row_copy(k, o).wait_recv()
        in_row = row_sums[k, 0]
        for i in range(1, n_row):
            in_row = in_row + row_sums[k, i]
        blk_sums[k, my_blk] = in_row
        each(n_blk - 1, lambda i: blk_copy(blk_sums, blk_send, blk_recv, k, i + 1).start())
        blk_wait(blk_sums, blk_recv, k)
        if n_blk <= 16:
            whole = blk_sums[k, 0]
            for i in range(1, n_blk):
                whole = whole + blk_sums[k, i]
        else:
            whole = jnp.sum(blk_sums[k], axis=0)

        curve, cross, square, data, norm = (whole[q : q + 1] for q in range(5))
        step = norm / curve
        norm_next = jnp.maximum(norm - 2.0 * step * cross + step * step * square, 0.0)
        turn = norm_next / norm
        quadratic_ref[...] = quadratic_ref[...] + step * data * (1.0 / tracers)

        def per_column(line):
            wide = jnp.broadcast_to(line, (columns, 128))
            kept = jnp.where(spread_row == spread_lane, wide, 0.0)
            return jnp.sum(kept, axis=1, keepdims=True)

        step_c, turn_c = per_column(step), per_column(turn)
        for l in range(leaves):
            d = direction[l]
            r = residual_ref[l] - step_c * applied[l]
            solution_ref[l] = solution_ref[l] + step_c * d
            residual_ref[l] = r
            direction[l] = r + turn_c * d

        for n in range(8):
            halo(k, n).wait_send()
        for o in range(1, n_row):
            row_copy(k, o).wait_send()
        blk_wait(skeletons, skel_send, k)
        blk_wait(blk_sums, blk_send, k)

    iteration(0, True)

    @pl.loop(1, ITERS)
    def _(k):
        iteration(k, False)


def local(
    n_row, n_blk,
    right_side, noise_level, near_blocks, skeleton_basis, skeleton_index, far_list, couplings,
):
    leaves, columns, width = right_side.shape[2:]
    rank = skeleton_basis.shape[3]
    field = jax.ShapeDtypeStruct((leaves, columns, width), jnp.float32)
    vmem = pl.BlockSpec(memory_space=pltpu.VMEM)
    dma = pltpu.SemaphoreType.DMA
    solution_out, residual_out, quadratic = pl.pallas_call(
        functools.partial(kernel, n_row, n_blk, n_row * n_blk * leaves * width),
        out_shape=(field, field, jax.ShapeDtypeStruct((1, 128), jnp.float32)),
        in_specs=[
            vmem, vmem, pl.BlockSpec(memory_space=pl.ANY), vmem, vmem,
            pl.BlockSpec(memory_space=pltpu.SMEM), vmem,
        ],
        out_specs=(vmem, vmem, vmem),
        scratch_shapes=[
            pltpu.VMEM(near_blocks.shape[2:], jnp.bfloat16),
            pltpu.VMEM((leaves, 3 * rank, width), jnp.bfloat16),
            pltpu.VMEM((ITERS, LEAF_ROWS + 2, LEAF_COLS + 2, columns, width), jnp.bfloat16),
            pltpu.VMEM((leaves, columns, width), jnp.float32),
            pltpu.VMEM((leaves, columns, width), jnp.float32),
            pltpu.VMEM((ITERS, n_blk, columns, rank), jnp.bfloat16),
            pltpu.VMEM((ITERS, n_row, 8, 128), jnp.float32),
            pltpu.VMEM((ITERS, n_blk, 8, 128), jnp.float32),
            dma((leaves,)),
            dma((ITERS, 8)), dma((ITERS, 8)),
            dma((ITERS,)), dma((ITERS,)),
            dma((ITERS, n_row - 1)), dma((ITERS, n_row - 1)),
            dma((ITERS,)), dma((ITERS,)),
        ],
        compiler_params=pltpu.CompilerParams(
            collective_id=0, has_side_effects=True, vmem_limit_bytes=48 * 1024 * 1024
        ),
    )(
        right_side[0, 0], noise_level[0, 0], near_blocks[0, 0], skeleton_basis[0, 0],
        skeleton_index[0], far_list[0], couplings[0, 0],
    )
    return solution_out[None, None], residual_out[None, None], quadratic[0, :columns]


def solution(mesh):
    return jax.shard_map(
        functools.partial(local, mesh.shape["row"], mesh.shape["blk"]),
        mesh=mesh,
        in_specs=(
            P("row", "blk", None, None, None),
            P("row", "blk", None, None),
            P("row", "blk", None, None, None, None),
            P("row", "blk", None, None, None),
            P("row", "blk", None),
            P("row", "blk", None),
            P("row", "blk", None, None, None),
        ),
        out_specs=(P("row", "blk", None, None, None), P("row", "blk", None, None, None), P()),
        check_vma=False,
    )
```

```python
import functools

import jax
import jax.numpy as jnp
from jax import lax
from jax.experimental import pallas as pl
from jax.experimental.pallas import tpu as pltpu
from jax.sharding import PartitionSpec as P

ITERS = 4
LEAF_ROWS = 2
LEAF_COLS = 4
MESH = pl.DeviceIdType.MESH
HIGHEST = lax.Precision.HIGHEST
SHIFTS = ((-1, 0), (1, 0), (0, -1), (0, 1), (-1, -1), (-1, 1), (1, -1), (1, 1))


def span(shift, count, incoming):
    if shift == 0:
        return 1, count
    if incoming:
        return (0 if shift > 0 else count + 1), 1
    return (count if shift > 0 else 1), 1


def each(count, body):
    if count <= 32:
        for i in range(count):
            body(i)
    else:
        pl.loop(0, count)(body)


def kernel(
    n_row, n_blk, tracers,
    right_hbm, noise_hbm, blocks_hbm, basis_hbm, index_ref, far_ref, coupling_hbm,
    solution_ref, residual_ref, quadratic_ref,
    right_ref, noise_ref, coupling_ref, blocks, mixed, extended, direction, applied, skeletons, sums_all,
    first_sem, load_sem, halo_send, halo_recv, skel_send, skel_recv, sum_send, sum_recv,
):
    leaves, columns, width = right_ref.shape
    rank = basis_hbm.shape[1]
    far_count = coupling_ref.shape[0]
    my_row, my_blk = lax.axis_index("row"), lax.axis_index("blk")

    firsts = [
        pltpu.make_async_copy(source, target, first_sem.at[i])
        for i, (source, target) in enumerate((
            (right_hbm, right_ref),
            (basis_hbm, mixed.at[:, pl.ds(0, rank)]),
            (noise_hbm, noise_ref),
            (coupling_hbm, coupling_ref),
        ))
    ]
    for first_load in firsts:
        first_load.start()
    loads = [
        pltpu.make_async_copy(blocks_hbm.at[l], blocks.at[l], load_sem.at[l]) for l in range(leaves)
    ]
    for load in loads:
        load.start()

    def row_at(o):
        return lax.rem(my_row + (o + n_row), n_row)

    def blk_at(o):
        return lax.rem(my_blk + (o + n_blk), n_blk)

    barrier = pltpu.get_barrier_semaphore()

    def greet(row, blk):
        pl.semaphore_signal(barrier, inc=1, device_id={"row": row, "blk": blk}, device_id_type=MESH)

    devices = n_row * n_blk
    each(devices - 1, lambda i: greet(row_at((i + 1) // n_blk), blk_at((i + 1) % n_blk)))

    sublane = lax.broadcasted_iota(jnp.int32, (rank, rank), 0)
    lane = lax.broadcasted_iota(jnp.int32, (rank, rank), 1)
    as_row = jnp.broadcast_to(index_ref[...].astype(jnp.float32), (rank, rank))
    as_column = jnp.sum(jnp.where(sublane == lane, as_row, 0.0), axis=1, keepdims=True)
    point = lax.broadcasted_iota(jnp.int32, (rank, width), 1).astype(jnp.float32)
    for l in range(leaves):
        picks = jnp.where(point + float(width * l) == as_column, 1.0, 0.0).astype(jnp.bfloat16)
        mixed[l, rank : 2 * rank] = picks
        mixed[l, 2 * rank :] = picks
    quadratic_ref[...] = jnp.zeros_like(quadratic_ref)
    for first_load in firsts:
        first_load.wait()
    for l in range(leaves):
        value = right_ref[l]
        direction[l] = value
        residual_ref[l] = value
        solution_ref[l] = jnp.zeros_like(value)

    pl.semaphore_wait(barrier, devices - 1)

    ones = jnp.ones((8, 128), jnp.float32)
    spread_row = lax.broadcasted_iota(jnp.int32, (columns, columns), 0)
    spread_lane = lax.broadcasted_iota(jnp.int32, (columns, columns), 1)

    def halo(k, n):
        dr, dc = SHIFTS[n]
        (sr, nr), (sc, nc) = span(dr, LEAF_ROWS, False), span(dc, LEAF_COLS, False)
        (tr, _), (tc, _) = span(dr, LEAF_ROWS, True), span(dc, LEAF_COLS, True)
        return pltpu.make_async_remote_copy(
            src_ref=extended.at[k, pl.ds(sr, nr), pl.ds(sc, nc)],
            dst_ref=extended.at[k, pl.ds(tr, nr), pl.ds(tc, nc)],
            send_sem=halo_send.at[k, n],
            recv_sem=halo_recv.at[k, n],
            device_id={"row": row_at(dr), "blk": blk_at(dc)},
            device_id_type=MESH,
        )

    me = my_row * n_blk + my_blk

    def sum_copy(k, i):
        return pltpu.make_async_remote_copy(
            src_ref=sums_all.at[k, me],
            dst_ref=sums_all.at[k, me],
            send_sem=sum_send.at[k],
            recv_sem=sum_recv.at[k],
            device_id={"row": row_at(i // n_blk), "blk": blk_at(i % n_blk)},
            device_id_type=MESH,
        )

    def blk_copy(buffer, send, recv, k, o):
        return pltpu.make_async_remote_copy(
            src_ref=buffer.at[k, my_blk],
            dst_ref=buffer.at[k, my_blk],
            send_sem=send.at[k],
            recv_sem=recv.at[k],
            device_id={"row": my_row, "blk": blk_at(o)},
            device_id_type=MESH,
        )

    def all_wait(buffer, sem, k, count):
        every = buffer.at[k, pl.ds(0, count - 1)]
        pltpu.make_async_copy(every, every, sem.at[k]).wait()

    def slots(l):
        a, c = divmod(l, LEAF_COLS)
        for s in range(9):
            yield s, a + s // 3, c + s % 3

    def inside(row, col):
        return 1 <= row <= LEAF_ROWS and 1 <= col <= LEAF_COLS

    def iteration(k, first):
        for l in range(leaves):
            a, c = divmod(l, LEAF_COLS)
            extended[k, a + 1, c + 1] = direction[l].astype(jnp.bfloat16)
        for n in range(8):
            halo(k, n).start()

        def field(row, col):
            return extended[k, row, col]

        both = jnp.zeros((columns, 2 * rank), jnp.float32)
        for l in range(leaves):
            a, c = divmod(l, LEAF_COLS)
            both = both + lax.dot_general(
                field(a + 1, c + 1), mixed[l, : 2 * rank], (((1,), (1,)), ((), ())),
                preferred_element_type=jnp.float32,
            )
        skeletons[k, my_blk] = (both[:, :rank] + both[:, rank:]).astype(jnp.bfloat16)
        each(n_blk - 1, lambda i: blk_copy(skeletons, skel_send, skel_recv, k, i + 1).start())

        for l in range(leaves):
            if first:
                loads[l].wait()
            total = noise_ref[l : l + 1] * direction[l]
            for s, row, col in slots(l):
                if inside(row, col):
                    total = total + jnp.dot(
                        field(row, col), blocks[l, s], preferred_element_type=jnp.float32
                    )
            applied[l] = total

        all_wait(skeletons, skel_recv, k, n_blk)
        far = jnp.zeros((columns, rank), jnp.float32)
        for j in range(far_count):
            far = far + jnp.dot(
                skeletons[k, far_ref[0, j]], coupling_ref[j], preferred_element_type=jnp.float32
            )
        far_high = far.astype(jnp.bfloat16)
        far_low = (far - far_high.astype(jnp.float32)).astype(jnp.bfloat16)
        far_all = jnp.concatenate([far_high, far_high, far_low], axis=1)

        for n in range(8):
            halo(k, n).wait_recv()

        sums = [jnp.zeros((columns, 128), jnp.float32) for _ in range(5)]
        for l in range(leaves):
            total = applied[l] + jnp.dot(far_all, mixed[l], preferred_element_type=jnp.float32)
            for s, row, col in slots(l):
                if not inside(row, col):
                    total = total + jnp.dot(
                        field(row, col), blocks[l, s], preferred_element_type=jnp.float32
                    )
            applied[l] = total
            d, r = direction[l], residual_ref[l]
            for q, product in enumerate((d * total, r * total, total * total, right_ref[l] * d, r * r)):
                for h in range(width // 128):
                    sums[q] = sums[q] + product[:, 128 * h : 128 * (h + 1)]

        rest = jnp.zeros((256 - 5 * columns, 128), jnp.float32)
        lines = lax.dot_general(
            ones, jnp.concatenate(sums + [rest], axis=0), (((1,), (1,)), ((), ())),
            precision=HIGHEST, preferred_element_type=jnp.float32,
        )
        sums_all[k, me] = lines[:1]
        each(devices - 1, lambda i: sum_copy(k, i + 1).start())
        all_wait(sums_all, sum_recv, k, devices)
        whole = jnp.sum(sums_all[k], axis=0)

        curve, cross, square, data, norm = (
            whole[:, q * columns : (q + 1) * columns] for q in range(5)
        )
        step = norm / curve
        norm_next = jnp.maximum(norm - 2.0 * step * cross + step * step * square, 0.0)
        turn = norm_next / norm
        quadratic_ref[...] = quadratic_ref[...] + step * data * (1.0 / tracers)

        def per_column(line):
            wide = jnp.broadcast_to(line, (columns, columns))
            kept = jnp.where(spread_row == spread_lane, wide, 0.0)
            return jnp.sum(kept, axis=1, keepdims=True)

        step_c, turn_c = per_column(step), per_column(turn)
        for l in range(leaves):
            d = direction[l]
            r = residual_ref[l] - step_c * applied[l]
            solution_ref[l] = solution_ref[l] + step_c * d
            residual_ref[l] = r
            direction[l] = r + turn_c * d

    iteration(0, True)

    @pl.loop(1, ITERS)
    def _(k):
        iteration(k, False)

    @pl.loop(0, ITERS)
    def _(k):
        for n in range(8):
            halo(k, n).wait_send()
        all_wait(skeletons, skel_send, k, n_blk)
        all_wait(sums_all, sum_send, k, devices)


def local(
    n_row, n_blk,
    right_side, noise_level, near_blocks, skeleton_basis, skeleton_index, far_list, couplings,
):
    leaves, columns, width = right_side.shape[2:]
    rank = skeleton_basis.shape[3]
    field = jax.ShapeDtypeStruct((leaves, columns, width), jnp.float32)
    vmem = pl.BlockSpec(memory_space=pltpu.VMEM)
    hbm = pl.BlockSpec(memory_space=pltpu.HBM)
    dma = pltpu.SemaphoreType.DMA
    solution_out, residual_out, quadratic = pl.pallas_call(
        functools.partial(kernel, n_row, n_blk, n_row * n_blk * leaves * width),
        out_shape=(field, field, jax.ShapeDtypeStruct((1, columns), jnp.float32)),
        in_specs=[
            hbm, hbm, hbm, hbm, vmem, pl.BlockSpec(memory_space=pltpu.SMEM), hbm,
        ],
        out_specs=(vmem, vmem, vmem),
        scratch_shapes=[
            pltpu.VMEM((leaves, columns, width), jnp.float32),
            pltpu.VMEM(noise_level.shape[2:], jnp.float32),
            pltpu.VMEM(couplings.shape[2:], jnp.bfloat16),
            pltpu.VMEM(near_blocks.shape[2:], jnp.bfloat16),
            pltpu.VMEM((leaves, 3 * rank, width), jnp.bfloat16),
            pltpu.VMEM((ITERS, LEAF_ROWS + 2, LEAF_COLS + 2, columns, width), jnp.bfloat16),
            pltpu.VMEM((leaves, columns, width), jnp.float32),
            pltpu.VMEM((leaves, columns, width), jnp.float32),
            pltpu.VMEM((ITERS, n_blk, columns, rank), jnp.bfloat16),
            pltpu.VMEM((ITERS, n_row * n_blk, 1, 256), jnp.float32),
            dma((4,)), dma((leaves,)),
            dma((ITERS, 8)), dma((ITERS, 8)),
            dma((ITERS,)), dma((ITERS,)),
            dma((ITERS,)), dma((ITERS,)),
        ],
        compiler_params=pltpu.CompilerParams(
            collective_id=0, has_side_effects=True, vmem_limit_bytes=48 * 1024 * 1024
        ),
    )(
        right_side[0, 0], noise_level[0, 0], near_blocks[0, 0], skeleton_basis[0, 0],
        skeleton_index[0], far_list[0], couplings[0, 0],
    )
    return solution_out[None, None], residual_out[None, None], quadratic[0]


def solution(mesh):
    return jax.shard_map(
        functools.partial(local, mesh.shape["row"], mesh.shape["blk"]),
        mesh=mesh,
        in_specs=(
            P("row", "blk", None, None, None),
            P("row", "blk", None, None),
            P("row", "blk", None, None, None, None),
            P("row", "blk", None, None, None),
            P("row", "blk", None),
            P("row", "blk", None),
            P("row", "blk", None, None, None),
        ),
        out_specs=(P("row", "blk", None, None, None), P("row", "blk", None, None, None), P()),
        check_vma=False,
    )
```

```python
import functools

import jax
import jax.numpy as jnp
from jax import lax
from jax.experimental import pallas as pl
from jax.experimental.pallas import tpu as pltpu
from jax.sharding import PartitionSpec as P

ITERS = 4
LEAF_ROWS = 2
LEAF_COLS = 4
MESH = pl.DeviceIdType.MESH
HIGHEST = lax.Precision.HIGHEST
SHIFTS = ((-1, 0), (1, 0), (0, -1), (0, 1), (-1, -1), (-1, 1), (1, -1), (1, 1))


def span(shift, count, incoming):
    if shift == 0:
        return 1, count
    if incoming:
        return (0 if shift > 0 else count + 1), 1
    return (count if shift > 0 else 1), 1


def each(count, body):
    if count <= 32:
        for i in range(count):
            body(i)
    else:
        pl.loop(0, count)(body)


def kernel(
    n_row, n_blk, tracers,
    right_hbm, noise_hbm, blocks_hbm, basis_hbm, index_ref, far_ref, coupling_hbm,
    solution_ref, residual_ref, quadratic_ref,
    right_ref, noise_ref, coupling_ref, blocks, mixed, extended, direction, applied, skeletons, sums_all,
    first_sem, load_sem, halo_send, halo_recv, skel_send, skel_recv, sum_send, sum_recv,
):
    leaves, columns, width = right_ref.shape
    rank = basis_hbm.shape[1]
    far_count = coupling_ref.shape[0]
    my_row, my_blk = lax.axis_index("row"), lax.axis_index("blk")

    firsts = [
        pltpu.make_async_copy(source, target, first_sem.at[i])
        for i, (source, target) in enumerate((
            (right_hbm, right_ref),
            (basis_hbm, mixed.at[:, pl.ds(0, rank)]),
            (noise_hbm, noise_ref),
            (coupling_hbm, coupling_ref),
        ))
    ]
    for first_load in firsts:
        first_load.start()
    loads = [
        pltpu.make_async_copy(blocks_hbm.at[l], blocks.at[l], load_sem.at[l]) for l in range(leaves)
    ]
    for load in loads:
        load.start()

    def row_at(o):
        return lax.rem(my_row + (o + n_row), n_row)

    def blk_at(o):
        return lax.rem(my_blk + (o + n_blk), n_blk)

    barrier = pltpu.get_barrier_semaphore()

    def greet(row, blk):
        pl.semaphore_signal(barrier, inc=1, device_id={"row": row, "blk": blk}, device_id_type=MESH)

    devices = n_row * n_blk
    each(devices - 1, lambda i: greet(row_at((i + 1) // n_blk), blk_at((i + 1) % n_blk)))

    sublane = lax.broadcasted_iota(jnp.int32, (rank, rank), 0)
    lane = lax.broadcasted_iota(jnp.int32, (rank, rank), 1)
    as_row = jnp.broadcast_to(index_ref[...].astype(jnp.float32), (rank, rank))
    as_column = jnp.sum(jnp.where(sublane == lane, as_row, 0.0), axis=1, keepdims=True)
    point = lax.broadcasted_iota(jnp.int32, (rank, width), 1).astype(jnp.float32)
    for l in range(leaves):
        picks = jnp.where(point + float(width * l) == as_column, 1.0, 0.0).astype(jnp.bfloat16)
        mixed[l, rank : 2 * rank] = picks
        mixed[l, 2 * rank :] = picks
    quadratic_ref[...] = jnp.zeros_like(quadratic_ref)
    for first_load in firsts:
        first_load.wait()
    for l in range(leaves):
        value = right_ref[l]
        direction[l] = value
        residual_ref[l] = value
        solution_ref[l] = jnp.zeros_like(value)

    pl.semaphore_wait(barrier, devices - 1)

    ones = jnp.ones((8, 128), jnp.float32)
    spread_row = lax.broadcasted_iota(jnp.int32, (columns, columns), 0)
    spread_lane = lax.broadcasted_iota(jnp.int32, (columns, columns), 1)

    def halo(k, n):
        dr, dc = SHIFTS[n]
        (sr, nr), (sc, nc) = span(dr, LEAF_ROWS, False), span(dc, LEAF_COLS, False)
        (tr, _), (tc, _) = span(dr, LEAF_ROWS, True), span(dc, LEAF_COLS, True)
        return pltpu.make_async_remote_copy(
            src_ref=extended.at[k, pl.ds(sr, nr), pl.ds(sc, nc)],
            dst_ref=extended.at[k, pl.ds(tr, nr), pl.ds(tc, nc)],
            send_sem=halo_send.at[k, n],
            recv_sem=halo_recv.at[k, n],
            device_id={"row": row_at(dr), "blk": blk_at(dc)},
            device_id_type=MESH,
        )

    me = my_row * n_blk + my_blk

    def sum_copy(k, i):
        return pltpu.make_async_remote_copy(
            src_ref=sums_all.at[k, me],
            dst_ref=sums_all.at[k, me],
            send_sem=sum_send.at[k],
            recv_sem=sum_recv.at[k],
            device_id={"row": row_at(i // n_blk), "blk": blk_at(i % n_blk)},
            device_id_type=MESH,
        )

    def blk_copy(buffer, send, recv, k, o):
        return pltpu.make_async_remote_copy(
            src_ref=buffer.at[k, my_blk],
            dst_ref=buffer.at[k, my_blk],
            send_sem=send.at[k],
            recv_sem=recv.at[k],
            device_id={"row": my_row, "blk": blk_at(o)},
            device_id_type=MESH,
        )

    def all_wait(buffer, sem, k, count):
        every = buffer.at[k, pl.ds(0, count - 1)]
        pltpu.make_async_copy(every, every, sem.at[k]).wait()

    def slots(l):
        a, c = divmod(l, LEAF_COLS)
        for s in range(9):
            yield s, a + s // 3, c + s % 3

    def inside(row, col):
        return 1 <= row <= LEAF_ROWS and 1 <= col <= LEAF_COLS

    def iteration(k, first):
        for l in range(leaves):
            a, c = divmod(l, LEAF_COLS)
            extended[k, a + 1, c + 1] = direction[l].astype(jnp.bfloat16)
        for n in range(8):
            halo(k, n).start()

        def field(row, col):
            return extended[k, row, col]

        both = jnp.zeros((columns, 2 * rank), jnp.float32)
        for l in range(leaves):
            a, c = divmod(l, LEAF_COLS)
            both = both + lax.dot_general(
                field(a + 1, c + 1), mixed[l, : 2 * rank], (((1,), (1,)), ((), ())),
                preferred_element_type=jnp.float32,
            )
        skeletons[k, my_blk] = (both[:, :rank] + both[:, rank:]).astype(jnp.bfloat16)
        each(n_blk - 1, lambda i: blk_copy(skeletons, skel_send, skel_recv, k, i + 1).start())

        for l in range(leaves):
            if first:
                loads[l].wait()
            total = noise_ref[l : l + 1] * direction[l]
            for s, row, col in slots(l):
                if inside(row, col):
                    total = total + jnp.dot(
                        field(row, col), blocks[l, s], preferred_element_type=jnp.float32
                    )
            applied[l] = total

        all_wait(skeletons, skel_recv, k, n_blk)
        far = jnp.zeros((columns, rank), jnp.float32)
        for j in range(far_count):
            far = far + jnp.dot(
                skeletons[k, far_ref[0, j]], coupling_ref[j], preferred_element_type=jnp.float32
            )
        far_high = far.astype(jnp.bfloat16)
        far_low = (far - far_high.astype(jnp.float32)).astype(jnp.bfloat16)
        far_all = jnp.concatenate([far_high, far_high, far_low], axis=1)

        for n in range(8):
            halo(k, n).wait_recv()

        sums = [jnp.zeros((columns, 128), jnp.float32) for _ in range(5)]
        for l in range(leaves):
            total = applied[l] + jnp.dot(far_all, mixed[l], preferred_element_type=jnp.float32)
            for s, row, col in slots(l):
                if not inside(row, col):
                    total = total + jnp.dot(
                        field(row, col), blocks[l, s], preferred_element_type=jnp.float32
                    )
            applied[l] = total
            d, r = direction[l], residual_ref[l]
            for q, product in enumerate((d * total, r * total, total * total, right_ref[l] * d, r * r)):
                for h in range(width // 128):
                    sums[q] = sums[q] + product[:, 128 * h : 128 * (h + 1)]

        rest = jnp.zeros((256 - 5 * columns, 128), jnp.float32)
        lines = lax.dot_general(
            ones, jnp.concatenate(sums + [rest], axis=0), (((1,), (1,)), ((), ())),
            precision=HIGHEST, preferred_element_type=jnp.float32,
        )
        sums_all[k, me] = lines[:1]
        each(devices - 1, lambda i: sum_copy(k, devices - 1 - i).start())
        all_wait(sums_all, sum_recv, k, devices)
        whole = jnp.sum(sums_all[k], axis=0)

        curve, cross, square, data, norm = (
            whole[:, q * columns : (q + 1) * columns] for q in range(5)
        )
        step = norm / curve
        norm_next = jnp.maximum(norm - 2.0 * step * cross + step * step * square, 0.0)
        turn = norm_next / norm
        quadratic_ref[...] = quadratic_ref[...] + step * data * (1.0 / tracers)

        def per_column(line):
            wide = jnp.broadcast_to(line, (columns, columns))
            kept = jnp.where(spread_row == spread_lane, wide, 0.0)
            return jnp.sum(kept, axis=1, keepdims=True)

        step_c, turn_c = per_column(step), per_column(turn)
        for l in range(leaves):
            d = direction[l]
            r = residual_ref[l] - step_c * applied[l]
            solution_ref[l] = solution_ref[l] + step_c * d
            residual_ref[l] = r
            direction[l] = r + turn_c * d

    iteration(0, True)

    @pl.loop(1, ITERS)
    def _(k):
        iteration(k, False)

    @pl.loop(0, ITERS)
    def _(k):
        for n in range(8):
            halo(k, n).wait_send()
        all_wait(skeletons, skel_send, k, n_blk)
        all_wait(sums_all, sum_send, k, devices)


def local(
    n_row, n_blk,
    right_side, noise_level, near_blocks, skeleton_basis, skeleton_index, far_list, couplings,
):
    leaves, columns, width = right_side.shape[2:]
    rank = skeleton_basis.shape[3]
    field = jax.ShapeDtypeStruct((leaves, columns, width), jnp.float32)
    vmem = pl.BlockSpec(memory_space=pltpu.VMEM)
    hbm = pl.BlockSpec(memory_space=pltpu.HBM)
    dma = pltpu.SemaphoreType.DMA
    solution_out, residual_out, quadratic = pl.pallas_call(
        functools.partial(kernel, n_row, n_blk, n_row * n_blk * leaves * width),
        out_shape=(field, field, jax.ShapeDtypeStruct((1, columns), jnp.float32)),
        in_specs=[
            hbm, hbm, hbm, hbm, vmem, pl.BlockSpec(memory_space=pltpu.SMEM), hbm,
        ],
        out_specs=(vmem, vmem, vmem),
        scratch_shapes=[
            pltpu.VMEM((leaves, columns, width), jnp.float32),
            pltpu.VMEM(noise_level.shape[2:], jnp.float32),
            pltpu.VMEM(couplings.shape[2:], jnp.bfloat16),
            pltpu.VMEM(near_blocks.shape[2:], jnp.bfloat16),
            pltpu.VMEM((leaves, 3 * rank, width), jnp.bfloat16),
            pltpu.VMEM((ITERS, LEAF_ROWS + 2, LEAF_COLS + 2, columns, width), jnp.bfloat16),
            pltpu.VMEM((leaves, columns, width), jnp.float32),
            pltpu.VMEM((leaves, columns, width), jnp.float32),
            pltpu.VMEM((ITERS, n_blk, columns, rank), jnp.bfloat16),
            pltpu.VMEM((ITERS, n_row * n_blk, 1, 256), jnp.float32),
            dma((4,)), dma((leaves,)),
            dma((ITERS, 8)), dma((ITERS, 8)),
            dma((ITERS,)), dma((ITERS,)),
            dma((ITERS,)), dma((ITERS,)),
        ],
        compiler_params=pltpu.CompilerParams(
            collective_id=0, has_side_effects=True, vmem_limit_bytes=63 * 1024 * 1024
        ),
    )(
        right_side[0, 0], noise_level[0, 0], near_blocks[0, 0], skeleton_basis[0, 0],
        skeleton_index[0], far_list[0], couplings[0, 0],
    )
    return solution_out[None, None], residual_out[None, None], quadratic[0]


def solution(mesh):
    return jax.shard_map(
        functools.partial(local, mesh.shape["row"], mesh.shape["blk"]),
        mesh=mesh,
        in_specs=(
            P("row", "blk", None, None, None),
            P("row", "blk", None, None),
            P("row", "blk", None, None, None, None),
            P("row", "blk", None, None, None),
            P("row", "blk", None),
            P("row", "blk", None),
            P("row", "blk", None, None, None),
        ),
        out_specs=(P("row", "blk", None, None, None), P("row", "blk", None, None, None), P()),
        check_vma=False,
    )
```

```python
import functools

import jax
import jax.numpy as jnp
from jax import lax
from jax.experimental import pallas as pl
from jax.experimental.pallas import tpu as pltpu
from jax.sharding import PartitionSpec as P

ITERS = 4
LEAF_ROWS = 2
LEAF_COLS = 4
MESH = pl.DeviceIdType.MESH
HIGHEST = lax.Precision.HIGHEST
SHIFTS = ((-1, 0), (1, 0), (0, -1), (0, 1), (-1, -1), (-1, 1), (1, -1), (1, 1))


def span(shift, count, incoming):
    if shift == 0:
        return 1, count
    if incoming:
        return (0 if shift > 0 else count + 1), 1
    return (count if shift > 0 else 1), 1


def each(count, body):
    if count <= 32:
        for i in range(count):
            body(i)
    else:
        pl.loop(0, count)(body)


def kernel(
    n_row, n_blk, tracers,
    right_hbm, noise_hbm, blocks_hbm, basis_hbm, index_ref, far_ref, coupling_hbm,
    solution_ref, residual_ref, quadratic_ref,
    right_ref, noise_ref, coupling_ref, blocks, mixed, extended, direction, applied, skeletons, sums_all,
    first_sem, load_sem, halo_send, halo_recv, skel_send, skel_recv, sum_send, sum_recv,
):
    leaves, columns, width = right_ref.shape
    rank = basis_hbm.shape[1]
    far_count = coupling_ref.shape[0]
    my_row, my_blk = lax.axis_index("row"), lax.axis_index("blk")

    firsts = [
        pltpu.make_async_copy(source, target, first_sem.at[i])
        for i, (source, target) in enumerate((
            (right_hbm, right_ref),
            (basis_hbm, mixed.at[:, pl.ds(0, rank)]),
            (noise_hbm, noise_ref),
            (coupling_hbm, coupling_ref),
        ))
    ]
    for first_load in firsts:
        first_load.start()
    loads = [
        pltpu.make_async_copy(blocks_hbm.at[l], blocks.at[l], load_sem.at[l]) for l in range(leaves)
    ]
    for load in loads:
        load.start()

    def row_at(o):
        return lax.rem(my_row + (o + n_row), n_row)

    def blk_at(o):
        return lax.rem(my_blk + (o + n_blk), n_blk)

    barrier = pltpu.get_barrier_semaphore()

    def greet(row, blk):
        pl.semaphore_signal(barrier, inc=1, device_id={"row": row, "blk": blk}, device_id_type=MESH)

    devices = n_row * n_blk
    each(devices - 1, lambda i: greet(row_at((i + 1) // n_blk), blk_at((i + 1) % n_blk)))

    sublane = lax.broadcasted_iota(jnp.int32, (rank, rank), 0)
    lane = lax.broadcasted_iota(jnp.int32, (rank, rank), 1)
    as_row = jnp.broadcast_to(index_ref[...].astype(jnp.float32), (rank, rank))
    as_column = jnp.sum(jnp.where(sublane == lane, as_row, 0.0), axis=1, keepdims=True)
    point = lax.broadcasted_iota(jnp.int32, (rank, width), 1).astype(jnp.float32)
    for l in range(leaves):
        picks = jnp.where(point + float(width * l) == as_column, 1.0, 0.0).astype(jnp.bfloat16)
        mixed[l, rank : 2 * rank] = picks
        mixed[l, 2 * rank :] = picks
    quadratic_ref[...] = jnp.zeros_like(quadratic_ref)
    for first_load in firsts:
        first_load.wait()
    for l in range(leaves):
        value = right_ref[l]
        direction[l] = value
        residual_ref[l] = value
        solution_ref[l] = jnp.zeros_like(value)

    pl.semaphore_wait(barrier, devices - 1)

    ones = jnp.ones((8, 128), jnp.float32)
    spread_row = lax.broadcasted_iota(jnp.int32, (columns, columns), 0)
    spread_lane = lax.broadcasted_iota(jnp.int32, (columns, columns), 1)

    def halo(k, n):
        dr, dc = SHIFTS[n]
        (sr, nr), (sc, nc) = span(dr, LEAF_ROWS, False), span(dc, LEAF_COLS, False)
        (tr, _), (tc, _) = span(dr, LEAF_ROWS, True), span(dc, LEAF_COLS, True)
        return pltpu.make_async_remote_copy(
            src_ref=extended.at[k, pl.ds(sr, nr), pl.ds(sc, nc)],
            dst_ref=extended.at[k, pl.ds(tr, nr), pl.ds(tc, nc)],
            send_sem=halo_send.at[k, n],
            recv_sem=halo_recv.at[k, n],
            device_id={"row": row_at(dr), "blk": blk_at(dc)},
            device_id_type=MESH,
        )

    me = my_row * n_blk + my_blk

    def sum_copy(k, i):
        return pltpu.make_async_remote_copy(
            src_ref=sums_all.at[k, me],
            dst_ref=sums_all.at[k, me],
            send_sem=sum_send.at[k],
            recv_sem=sum_recv.at[k],
            device_id={"row": row_at(i // n_blk), "blk": blk_at(i % n_blk)},
            device_id_type=MESH,
        )

    def blk_copy(buffer, send, recv, k, o):
        return pltpu.make_async_remote_copy(
            src_ref=buffer.at[k, my_blk],
            dst_ref=buffer.at[k, my_blk],
            send_sem=send.at[k],
            recv_sem=recv.at[k],
            device_id={"row": my_row, "blk": blk_at(o)},
            device_id_type=MESH,
        )

    def all_wait(buffer, sem, k, count):
        every = buffer.at[k, pl.ds(0, count - 1)]
        pltpu.make_async_copy(every, every, sem.at[k]).wait()

    def slots(l):
        a, c = divmod(l, LEAF_COLS)
        for s in range(9):
            yield s, a + s // 3, c + s % 3

    def inside(row, col):
        return 1 <= row <= LEAF_ROWS and 1 <= col <= LEAF_COLS

    def iteration(k, first):
        for l in range(leaves):
            a, c = divmod(l, LEAF_COLS)
            extended[k, a + 1, c + 1] = direction[l].astype(jnp.bfloat16)
        for n in range(8):
            halo(k, n).start()

        def field(row, col):
            return extended[k, row, col]

        both = jnp.zeros((columns, 2 * rank), jnp.float32)
        for l in range(leaves):
            a, c = divmod(l, LEAF_COLS)
            both = both + lax.dot_general(
                field(a + 1, c + 1), mixed[l, : 2 * rank], (((1,), (1,)), ((), ())),
                preferred_element_type=jnp.float32,
            )
        skeletons[k, my_blk] = (both[:, :rank] + both[:, rank:]).astype(jnp.bfloat16)
        each(n_blk - 1, lambda i: blk_copy(skeletons, skel_send, skel_recv, k, i + 1).start())

        for l in range(leaves):
            if first:
                loads[l].wait()
            total = noise_ref[l : l + 1] * direction[l]
            for s, row, col in slots(l):
                if inside(row, col):
                    total = total + jnp.dot(
                        field(row, col), blocks[l, s], preferred_element_type=jnp.float32
                    )
            applied[l] = total

        sums = [jnp.zeros((columns, 128), jnp.float32) for _ in range(5)]

        def add(q, product):
            for h in range(width // 128):
                sums[q] = sums[q] + product[:, 128 * h : 128 * (h + 1)]

        for l in range(leaves):
            add(3, right_ref[l] * direction[l])
            add(4, residual_ref[l] * residual_ref[l])

        all_wait(skeletons, skel_recv, k, n_blk)
        far = jnp.zeros((columns, rank), jnp.float32)
        for j in range(far_count):
            far = far + jnp.dot(
                skeletons[k, far_ref[0, j]], coupling_ref[j], preferred_element_type=jnp.float32
            )
        far_high = far.astype(jnp.bfloat16)
        far_low = (far - far_high.astype(jnp.float32)).astype(jnp.bfloat16)
        far_all = jnp.concatenate([far_high, far_high, far_low], axis=1)

        for n in range(8):
            halo(k, n).wait_recv()

        for l in range(leaves):
            total = applied[l] + jnp.dot(far_all, mixed[l], preferred_element_type=jnp.float32)
            for s, row, col in slots(l):
                if not inside(row, col):
                    total = total + jnp.dot(
                        field(row, col), blocks[l, s], preferred_element_type=jnp.float32
                    )
            applied[l] = total
            d, r = direction[l], residual_ref[l]
            add(0, d * total)
            add(1, r * total)
            add(2, total * total)

        rest = jnp.zeros((256 - 5 * columns, 128), jnp.float32)
        lines = lax.dot_general(
            ones, jnp.concatenate(sums + [rest], axis=0), (((1,), (1,)), ((), ())),
            precision=HIGHEST, preferred_element_type=jnp.float32,
        )
        sums_all[k, me] = lines[:1]
        each(devices - 1, lambda i: sum_copy(k, devices - 1 - i).start())
        all_wait(sums_all, sum_recv, k, devices)
        whole = jnp.sum(sums_all[k], axis=0)

        curve, cross, square, data, norm = (
            whole[:, q * columns : (q + 1) * columns] for q in range(5)
        )
        step = norm / curve
        norm_next = jnp.maximum(norm - 2.0 * step * cross + step * step * square, 0.0)
        turn = norm_next / norm
        quadratic_ref[...] = quadratic_ref[...] + step * data * (1.0 / tracers)

        def per_column(line):
            wide = jnp.broadcast_to(line, (columns, columns))
            kept = jnp.where(spread_row == spread_lane, wide, 0.0)
            return jnp.sum(kept, axis=1, keepdims=True)

        step_c, turn_c = per_column(step), per_column(turn)
        for l in range(leaves):
            d = direction[l]
            r = residual_ref[l] - step_c * applied[l]
            solution_ref[l] = solution_ref[l] + step_c * d
            residual_ref[l] = r
            direction[l] = r + turn_c * d

    iteration(0, True)

    @pl.loop(1, ITERS)
    def _(k):
        iteration(k, False)

    @pl.loop(0, ITERS)
    def _(k):
        for n in range(8):
            halo(k, n).wait_send()
        all_wait(skeletons, skel_send, k, n_blk)
        all_wait(sums_all, sum_send, k, devices)


def local(
    n_row, n_blk,
    right_side, noise_level, near_blocks, skeleton_basis, skeleton_index, far_list, couplings,
):
    leaves, columns, width = right_side.shape[2:]
    rank = skeleton_basis.shape[3]
    field = jax.ShapeDtypeStruct((leaves, columns, width), jnp.float32)
    vmem = pl.BlockSpec(memory_space=pltpu.VMEM)
    hbm = pl.BlockSpec(memory_space=pltpu.HBM)
    dma = pltpu.SemaphoreType.DMA
    solution_out, residual_out, quadratic = pl.pallas_call(
        functools.partial(kernel, n_row, n_blk, n_row * n_blk * leaves * width),
        out_shape=(field, field, jax.ShapeDtypeStruct((1, columns), jnp.float32)),
        in_specs=[
            hbm, hbm, hbm, hbm, vmem, pl.BlockSpec(memory_space=pltpu.SMEM), hbm,
        ],
        out_specs=(vmem, vmem, vmem),
        scratch_shapes=[
            pltpu.VMEM((leaves, columns, width), jnp.float32),
            pltpu.VMEM(noise_level.shape[2:], jnp.float32),
            pltpu.VMEM(couplings.shape[2:], jnp.bfloat16),
            pltpu.VMEM(near_blocks.shape[2:], jnp.bfloat16),
            pltpu.VMEM((leaves, 3 * rank, width), jnp.bfloat16),
            pltpu.VMEM((ITERS, LEAF_ROWS + 2, LEAF_COLS + 2, columns, width), jnp.bfloat16),
            pltpu.VMEM((leaves, columns, width), jnp.float32),
            pltpu.VMEM((leaves, columns, width), jnp.float32),
            pltpu.VMEM((ITERS, n_blk, columns, rank), jnp.bfloat16),
            pltpu.VMEM((ITERS, n_row * n_blk, 1, 256), jnp.float32),
            dma((4,)), dma((leaves,)),
            dma((ITERS, 8)), dma((ITERS, 8)),
            dma((ITERS,)), dma((ITERS,)),
            dma((ITERS,)), dma((ITERS,)),
        ],
        compiler_params=pltpu.CompilerParams(
            collective_id=0, has_side_effects=True, vmem_limit_bytes=63 * 1024 * 1024
        ),
    )(
        right_side[0, 0], noise_level[0, 0], near_blocks[0, 0], skeleton_basis[0, 0],
        skeleton_index[0], far_list[0], couplings[0, 0],
    )
    return solution_out[None, None], residual_out[None, None], quadratic[0]


def solution(mesh):
    return jax.shard_map(
        functools.partial(local, mesh.shape["row"], mesh.shape["blk"]),
        mesh=mesh,
        in_specs=(
            P("row", "blk", None, None, None),
            P("row", "blk", None, None),
            P("row", "blk", None, None, None, None),
            P("row", "blk", None, None, None),
            P("row", "blk", None),
            P("row", "blk", None),
            P("row", "blk", None, None, None),
        ),
        out_specs=(P("row", "blk", None, None, None), P("row", "blk", None, None, None), P()),
        check_vma=False,
    )
```
